32 devices in a mesh: groups: 2 (over y), seq: 4 (over z), head: 2 (over x), tile: 2 (over core).
Axes of the slice: x: 2, y: 2, z: 4, core: 2. Of those that a mesh axis runs over, the one named last changes fastest.
Arguments:
- query_states: bfloat16 [4608, 3072], P(('groups', 'seq', 'tile'), 'head'), parts along dimension 0, may hold values from -5 to 5
- key_states: bfloat16 [4608, 3072], P(('groups', 'seq', 'tile'), 'head'), parts along dimension 0, may hold values from -5 to 5
- value_states: bfloat16 [4608, 3072], P(('groups', 'seq', 'tile'), 'head'), parts along dimension 0, may hold values from -6 to 6
- residual: bfloat16 [4608, 3072], P(('groups', 'seq', 'tile'), 'head'), parts along dimension 0, may hold values from -6 to 6
- out_weight: bfloat16 [3072, 3072], P(None, 'head'), may hold values from -0.109375 to 0.109375
- gate_scale: float32 [6144], P(('groups', 'head')), parts along dimension 0, may hold values from 2 to 8
Outputs:
- block_out: bfloat16 [4608, 3072], P(('groups', 'seq', 'tile'), 'head'), parts along dimension 0
The draws below stay inside these ranges and needn't reach their ends.
There are 2 independent parts, one for each index of `groups`. The reference program is written for one: setup_inputs(seed, part) draws one part's arguments, and reference() takes and returns one part's arrays. A program takes and returns all parts, laid end to end along the dimension named above; an argument that names none is the same for every part. Nothing has to cross between parts.
All inputs are finite; a program needn't handle non-finite values.
Results may differ from the reference program's by a relative error of at most 0.0065.
Values may be sent and summed in bfloat16 or wider, within the bound.
A program may use at most 128 MiB of HBM per device.

```python
import math
import jax
import jax.numpy as jnp
from jax import lax

D = 3072
HEADS = 24
HD = 128
SEQ = 2304


def draw_query_states(key, part):
    values_out = 1.4 * jax.random.truncated_normal(jax.random.fold_in(key, 1), -5.0 / 1.4, 5.0 / 1.4, (SEQ, D), jnp.float32)
    return values_out.astype(jnp.bfloat16)


def draw_key_states(key, part):
    values_out = 1.4 * jax.random.truncated_normal(jax.random.fold_in(key, 2), -5.0 / 1.4, 5.0 / 1.4, (SEQ, D), jnp.float32)
    return values_out.astype(jnp.bfloat16)


def shard_levels(rng, dims, split, low, high):
    factor_of = 1.0
    for axis_at, shards_of in split:
        steps = jax.random.uniform(jax.random.fold_in(jax.random.fold_in(rng, 6), axis_at), (shards_of,), jnp.float32, low / len(split), high / len(split))
        factor_of = factor_of * jnp.repeat(jnp.exp(steps), dims[axis_at] // shards_of).reshape((-1,) + (1,) * (len(dims) - 1 - axis_at))
    return factor_of


def scatter_about(stream_key, extent, spread, bound, split=(), held_as=jnp.bfloat16):
    result = spread * jax.random.normal(stream_key, extent, jnp.float32)
    if split:
        result = result * shard_levels(stream_key, extent, split, -0.22, 0.18)
    return jnp.clip(result, -bound, bound).astype(held_as)


def setup_inputs(seed: int = 0, part: int = 0) -> dict:
    splits = jax.random.split(jax.random.key(seed), 7)
    own_keys = jax.random.split(jax.random.fold_in(splits[6], part), 7)
    return {
        "query_states": draw_query_states(jax.random.fold_in(jax.random.fold_in(splits[6], part), 71), part),
        "key_states": draw_key_states(jax.random.fold_in(jax.random.fold_in(splits[6], part), 71), part),
        "value_states": scatter_about(own_keys[2], (SEQ, D), 1.0, 6.0, ((0, 8), (1, 2))),
        "residual": scatter_about(own_keys[3], (SEQ, D), 1.0, 6.0, ((0, 8), (1, 2))),
        "out_weight": scatter_about(splits[4], (D, D), D ** -0.5, 0.109375, ((1, 2),)),
        "gate_scale": jnp.clip(jnp.exp(math.log(8.0) - 1.3862944 * jax.random.uniform(own_keys[5], (D,), jnp.float32) ** shard_levels(own_keys[5], (D,), ((0, 2),), -0.2, 0.2)), 2.0, 8.0),
    }


def reference(query_states, key_states, value_states, residual, out_weight, gate_scale):
    score_scale = 1.0 / math.sqrt(HD)
    block_rows = math.gcd(SEQ, 1024)

    def one_head(head_index):
        query_head = lax.dynamic_slice_in_dim(query_states, head_index * HD, HD, 1)
        key_head = lax.dynamic_slice_in_dim(key_states, head_index * HD, HD, 1).astype(jnp.float32)
        value_head = lax.dynamic_slice_in_dim(value_states, head_index * HD, HD, 1)
        value_wide = value_head.astype(jnp.float32)

        def one_block(query_block):
            scores = jnp.dot(query_block.astype(jnp.float32), key_head.T, preferred_element_type=jnp.float32) * score_scale
            row_max = lax.optimization_barrier(jnp.max(scores, axis=1, keepdims=True))
            weights = jnp.exp(scores - row_max)
            denominator = lax.optimization_barrier(jnp.sum(weights, axis=1, keepdims=True))
            probs = weights.astype(jnp.bfloat16).astype(jnp.float32)
            summed = jnp.dot(probs, value_wide, preferred_element_type=jnp.float32)
            return (summed / denominator).astype(jnp.bfloat16)
        blocks = query_head.reshape(SEQ // block_rows, block_rows, HD)
        return lax.map(one_block, blocks).reshape(SEQ, HD)
    per_head = lax.map(one_head, jnp.arange(HEADS, dtype=jnp.int32))
    attended = jnp.transpose(per_head, (1, 0, 2)).reshape(SEQ, D)
    projected = jnp.dot(attended, out_weight, preferred_element_type=jnp.float32)
    return (residual.astype(jnp.float32) + gate_scale[None, :] * projected).astype(jnp.bfloat16)
```

```python
import functools
import math

import jax
import jax.numpy as jnp
from jax import lax
from jax.experimental import pallas as pl
from jax.experimental.pallas import tpu as pltpu
from jax.sharding import PartitionSpec as P

HD = 128
MESH = pl.DeviceIdType.MESH


def gathered(query_states, key_states, value_states, residual, out_weight, gate_scale):
    row_count = query_states.shape[0]
    heads_here = query_states.shape[1] // HD
    score_scale = 1.0 / math.sqrt(HD)
    query_heads = query_states.reshape(row_count, heads_here, HD)
    key_heads = lax.all_gather(key_states, ("seq", "tile"), axis=0, tiled=True).reshape(
        -1, heads_here, HD
    )
    value_heads = lax.all_gather(value_states, ("seq", "tile"), axis=0, tiled=True).reshape(
        -1, heads_here, HD
    )
    scores = (
        jnp.einsum("qhd,khd->hqk", query_heads, key_heads, preferred_element_type=jnp.float32)
        * score_scale
    )
    row_max = jnp.max(scores, axis=2)
    weights = jnp.exp(scores - row_max[:, :, None])
    denominator = jnp.sum(weights, axis=2)
    numerator = jnp.einsum(
        "hqk,khd->qhd",
        weights.astype(jnp.bfloat16),
        value_heads,
        preferred_element_type=jnp.float32,
    )
    attended = (
        (numerator / denominator.T[:, :, None])
        .astype(jnp.bfloat16)
        .reshape(row_count, heads_here * HD)
    )
    projected = jnp.dot(
        lax.all_gather(attended, "head", axis=1, tiled=True),
        out_weight,
        preferred_element_type=jnp.float32,
    )
    return (residual.astype(jnp.float32) + gate_scale[None, :] * projected).astype(jnp.bfloat16)


def kernel(
    n,
    nx,
    per_chip,
    q_hbm,
    k_hbm,
    v_hbm,
    res_hbm,
    w_hbm,
    gate_ref,
    out_ref,
    q_out,
    kv_out,
    q_in,
    kv_in,
    o_out,
    att,
    w_buf,
    res_buf,
    acc,
    load_sem,
    w_sem,
    res_sem,
    q_send,
    q_recv,
    kv_send,
    kv_recv,
    fwd_send,
    fwd_recv,
    o_send,
    o_recv,
    x_send,
    x_recv,
):
    z = lax.axis_index("seq")
    x = lax.axis_index("head")
    c = lax.axis_index("tile")
    rows = q_hbm.shape[0]
    columns = w_hbm.shape[1]
    heads_here = n * per_chip

    def ahead(d):
        return lax.rem(z + d, n)

    def behind(d):
        return lax.rem(z - d + n, n)

    def x_ahead(f):
        return lax.rem(x + f, nx)

    def x_behind(f):
        return lax.rem(x - f + nx, nx)

    def slot(s):
        return pl.ds(s * rows, rows)

    loads = {}
    for j in range(per_chip):
        for d in range(n):
            cols = pl.ds(pl.multiple_of((ahead(d) * per_chip + j) * HD, HD), HD)
            if d == 0:
                dsts = (q_in.at[j, 0], kv_in.at[j, 0, slot(0)], kv_in.at[j, 1, slot(0)])
            else:
                dsts = (q_out.at[j, d], kv_out.at[j, d, 0], kv_out.at[j, d, 1])
            for t, (src, dst) in enumerate(zip((q_hbm, k_hbm, v_hbm), dsts)):
                copy = pltpu.make_async_copy(src.at[:, cols], dst, load_sem.at[t, j, d])
                copy.start()
                loads[t, j, d] = copy

    barrier = pltpu.get_barrier_semaphore()
    for d in range(1, n):
        pl.semaphore_signal(barrier, inc=1, device_id={"seq": ahead(d)}, device_id_type=MESH)
    for f in range(1, nx):
        pl.semaphore_signal(barrier, inc=1, device_id={"head": x_ahead(f)}, device_id_type=MESH)
    pl.semaphore_signal(barrier, inc=1, device_id={"tile": 1 - c}, device_id_type=MESH)
    pl.semaphore_wait(barrier, n + nx - 1)

    def q_copy(j, d):
        return pltpu.make_async_remote_copy(
            src_ref=q_out.at[j, d],
            dst_ref=q_in.at[j, d],
            send_sem=q_send.at[j, d],
            recv_sem=q_recv.at[j, d],
            device_id={"seq": ahead(d)},
            device_id_type=MESH,
        )

    def kv_copy(j, d):
        return pltpu.make_async_remote_copy(
            src_ref=kv_out.at[j, d],
            dst_ref=kv_in.at[j, :, slot(2 * d)],
            send_sem=kv_send.at[j, d],
            recv_sem=kv_recv.at[j, d],
            device_id={"seq": ahead(d)},
            device_id_type=MESH,
        )

    def fwd_copy(j, d):
        return pltpu.make_async_remote_copy(
            src_ref=kv_in.at[j, :, slot(2 * d)],
            dst_ref=kv_in.at[j, :, slot(2 * d + 1)],
            send_sem=fwd_send.at[j, d],
            recv_sem=fwd_recv.at[j, d],
            device_id={"tile": 1 - c},
            device_id_type=MESH,
        )

    def o_copy(j, d):
        return pltpu.make_async_remote_copy(
            src_ref=o_out.at[j, d],
            dst_ref=att.at[j, d],
            send_sem=o_send.at[j, d],
            recv_sem=o_recv.at[j, d],
            device_id={"seq": behind(d)},
            device_id_type=MESH,
        )

    def x_copy(j, f, d):
        return pltpu.make_async_remote_copy(
            src_ref=att.at[j, d],
            dst_ref=att.at[j, f * n + d],
            send_sem=x_send.at[j, f, d],
            recv_sem=x_recv.at[j, f, d],
            device_id={"head": x_ahead(f)},
            device_id_type=MESH,
        )

    for j in range(per_chip):
        for d in range(n - 1, 0, -1):
            loads[1, j, d].wait()
            loads[2, j, d].wait()
            kv_copy(j, d).start()
            loads[0, j, d].wait()
            q_copy(j, d).start()
        for t in range(3):
            loads[t, j, 0].wait()
        fwd_copy(j, 0).start()

    w_loads = {}
    for j in range(per_chip):
        for f in range(nx):
            for d in range(n):
                head = x_behind(f) * heads_here + ahead(d) * per_chip + j
                copy = pltpu.make_async_copy(
                    w_hbm.at[pl.ds(pl.multiple_of(head * HD, HD), HD)],
                    w_buf.at[j, pl.ds((f * n + d) * HD, HD)],
                    w_sem.at[j, f * n + d],
                )
                copy.start()
                w_loads[j, f, d] = copy
    res_load = pltpu.make_async_copy(res_hbm, res_buf, res_sem)
    res_load.start()

    factor = math.log2(math.e) / math.sqrt(HD)

    def attend(j, d):
        scores = lax.dot_general(
            q_in[j, d],
            kv_in[j, 0],
            (((1,), (1,)), ((), ())),
            preferred_element_type=jnp.float32,
        )
        row_max = jnp.max(scores, axis=1, keepdims=True)
        weights = jnp.exp2((scores - row_max) * factor)
        denominator = jnp.sum(weights, axis=1, keepdims=True)
        numerator = jnp.dot(
            weights.astype(jnp.bfloat16), kv_in[j, 1], preferred_element_type=jnp.float32
        )
        return (numerator / denominator).astype(jnp.bfloat16)

    def relay(j):
        for d in range(n):
            if d:
                o_copy(j, d).wait_recv()
            for f in range(1, nx):
                x_copy(j, f, d).start()

    width = math.gcd(columns, 512)

    def project(j):
        for f in range(nx):
            for d in range(n):
                w_loads[j, f, d].wait()
                if f:
                    x_copy(j, f, d).wait_recv()
        if j == per_chip - 1:
            res_load.wait()
        rows_in = jnp.concatenate([att[j, s] for s in range(nx * n)], axis=1)
        for start in range(0, columns, width):
            cols = slice(start, start + width)
            part = jnp.dot(rows_in, w_buf[j, :, cols], preferred_element_type=jnp.float32)
            if j:
                part += acc[:, cols]
            if j < per_chip - 1:
                acc[:, cols] = part
            else:
                out_ref[:, cols] = (
                    res_buf[:, cols].astype(jnp.float32) + gate_ref[:, cols] * part
                ).astype(jnp.bfloat16)

    for j in range(per_chip):
        for d in range(1, n):
            kv_copy(j, d).wait_recv()
            fwd_copy(j, d).start()
        for d in range(n):
            fwd_copy(j, d).wait_recv()
        for d in range(1, n):
            q_copy(j, d).wait_recv()
        if j:
            relay(j - 1)

        def step(i, carry):
            d = n - 1 - i
            o_out[j, d] = attend(j, d)

            @pl.when(d > 0)
            def _():
                o_copy(j, d).start()

            return carry

        lax.fori_loop(0, n, step, 0)
        att[j, 0] = o_out[j, 0]
        if j:
            project(j - 1)
    relay(per_chip - 1)
    project(per_chip - 1)

    for j in range(per_chip):
        for d in range(n):
            fwd_copy(j, d).wait_send()
            if d:
                q_copy(j, d).wait_send()
                kv_copy(j, d).wait_send()
                o_copy(j, d).wait_send()
            for f in range(1, nx):
                x_copy(j, f, d).wait_send()


def exchanged(n, nx, query_states, key_states, value_states, residual, out_weight, gate_scale):
    rows, width = query_states.shape
    columns = out_weight.shape[1]
    per_chip = width // HD // n
    bf16 = jnp.bfloat16
    dma = pltpu.SemaphoreType.DMA
    anywhere = pl.BlockSpec(memory_space=pl.ANY)
    in_vmem = pl.BlockSpec(memory_space=pltpu.VMEM)
    return pl.pallas_call(
        functools.partial(kernel, n, nx, per_chip),
        out_shape=jax.ShapeDtypeStruct((rows, columns), bf16),
        in_specs=[anywhere] * 5 + [in_vmem],
        out_specs=in_vmem,
        scratch_shapes=[
            pltpu.VMEM((per_chip, n, rows, HD), bf16),
            pltpu.VMEM((per_chip, n, 2, rows, HD), bf16),
            pltpu.VMEM((per_chip, n, rows, HD), bf16),
            pltpu.VMEM((per_chip, 2, 2 * n * rows, HD), bf16),
            pltpu.VMEM((per_chip, n, rows, HD), bf16),
            pltpu.VMEM((per_chip, nx * n, rows, HD), bf16),
            pltpu.VMEM((per_chip, nx * n * HD, columns), bf16),
            pltpu.VMEM((rows, columns), bf16),
            pltpu.VMEM((rows, columns), jnp.float32),
            dma((3, per_chip, n)),
            dma((per_chip, nx * n)),
            dma,
            dma((per_chip, n)),
            dma((per_chip, n)),
            dma((per_chip, n)),
            dma((per_chip, n)),
            dma((per_chip, n)),
            dma((per_chip, n)),
            dma((per_chip, n)),
            dma((per_chip, n)),
            dma((per_chip, nx, n)),
            dma((per_chip, nx, n)),
        ],
        compiler_params=pltpu.CompilerParams(
            collective_id=0, has_side_effects=True, vmem_limit_bytes=56 << 20
        ),
    )(query_states, key_states, value_states, residual, out_weight, gate_scale[None, :])


def solution(mesh):
    n, nx = mesh.shape["seq"], mesh.shape["head"]

    def per_device(query_states, *rest):
        heads_here = query_states.shape[1] // HD
        if heads_here % n or mesh.shape["tile"] != 2:
            return gathered(query_states, *rest)
        return exchanged(n, nx, query_states, *rest)

    placed = (
        P(("groups", "seq", "tile"), "head"),
        P(("groups", "seq", "tile"), "head"),
        P(("groups", "seq", "tile"), "head"),
        P(("groups", "seq", "tile"), "head"),
        P(None, "head"),
        P(("groups", "head")),
    )
    return jax.shard_map(
        per_device,
        mesh=mesh,
        in_specs=placed,
        out_specs=P(("groups", "seq", "tile"), "head"),
        check_vma=False,
    )
```

```python
import functools
import math

import jax
import jax.numpy as jnp
from jax import lax
from jax.experimental import pallas as pl
from jax.experimental.pallas import tpu as pltpu
from jax.sharding import PartitionSpec as P

HD = 128
MESH = pl.DeviceIdType.MESH


def gathered(query_states, key_states, value_states, residual, out_weight, gate_scale):
    row_count = query_states.shape[0]
    heads_here = query_states.shape[1] // HD
    score_scale = 1.0 / math.sqrt(HD)
    query_heads = query_states.reshape(row_count, heads_here, HD)
    key_heads = lax.all_gather(key_states, ("seq", "tile"), axis=0, tiled=True).reshape(
        -1, heads_here, HD
    )
    value_heads = lax.all_gather(value_states, ("seq", "tile"), axis=0, tiled=True).reshape(
        -1, heads_here, HD
    )
    scores = (
        jnp.einsum("qhd,khd->hqk", query_heads, key_heads, preferred_element_type=jnp.float32)
        * score_scale
    )
    row_max = jnp.max(scores, axis=2)
    weights = jnp.exp(scores - row_max[:, :, None])
    denominator = jnp.sum(weights, axis=2)
    numerator = jnp.einsum(
        "hqk,khd->qhd",
        weights.astype(jnp.bfloat16),
        value_heads,
        preferred_element_type=jnp.float32,
    )
    attended = (
        (numerator / denominator.T[:, :, None])
        .astype(jnp.bfloat16)
        .reshape(row_count, heads_here * HD)
    )
    projected = jnp.dot(
        lax.all_gather(attended, "head", axis=1, tiled=True),
        out_weight,
        preferred_element_type=jnp.float32,
    )
    return (residual.astype(jnp.float32) + gate_scale[None, :] * projected).astype(jnp.bfloat16)


def kernel(
    n,
    nx,
    per_chip,
    q_hbm,
    k_hbm,
    v_hbm,
    w_hbm,
    out_ref,
    q_out,
    kv_out,
    q_in,
    kv_in,
    o_out,
    att,
    w_buf,
    load_sem,
    w_sem,
    q_send,
    q_recv,
    kv_send,
    kv_recv,
    fwd_send,
    fwd_recv,
    o_send,
    o_recv,
    x_send,
    x_recv,
):
    z = lax.axis_index("seq")
    x = lax.axis_index("head")
    c = lax.axis_index("tile")
    rows = q_hbm.shape[0]
    columns = w_hbm.shape[1]
    heads_here = n * per_chip
    bits = [1 << b for b in range(n.bit_length() - 1)]
    order = list(range(n - 1, 0, -1))

    def partner(d):
        return sum(b * (((z // b) + (d // b)) % 2) for b in bits)

    def x_ahead(f):
        return lax.rem(x + f, nx)

    def x_behind(f):
        return lax.rem(x - f + nx, nx)

    def slot(s):
        return pl.ds(s * rows, rows)

    loads = {}
    for j in range(per_chip):
        for d in range(n):
            cols = pl.ds(pl.multiple_of((partner(d) * per_chip + j) * HD, HD), HD)
            if d == 0:
                dsts = (q_in.at[j, 0], kv_in.at[j, 0, slot(0)], kv_in.at[j, 1, slot(0)])
            else:
                dsts = (q_out.at[j, d], kv_out.at[j, d, 0], kv_out.at[j, d, 1])
            for t, (src, dst) in enumerate(zip((q_hbm, k_hbm, v_hbm), dsts)):
                copy = pltpu.make_async_copy(src.at[:, cols], dst, load_sem.at[t, j, d])
                copy.start()
                loads[t, j, d] = copy

    barrier = pltpu.get_barrier_semaphore()
    for d in range(1, n):
        pl.semaphore_signal(barrier, inc=1, device_id={"seq": partner(d)}, device_id_type=MESH)
    for f in range(1, nx):
        pl.semaphore_signal(barrier, inc=1, device_id={"head": x_ahead(f)}, device_id_type=MESH)
    pl.semaphore_signal(barrier, inc=1, device_id={"tile": 1 - c}, device_id_type=MESH)
    pl.semaphore_wait(barrier, n + nx - 1)

    def q_copy(j, d):
        return pltpu.make_async_remote_copy(
            src_ref=q_out.at[j, d],
            dst_ref=q_in.at[j, d],
            send_sem=q_send.at[j, d],
            recv_sem=q_recv.at[j, d],
            device_id={"seq": partner(d)},
            device_id_type=MESH,
        )

    def kv_copy(j, d):
        return pltpu.make_async_remote_copy(
            src_ref=kv_out.at[j, d],
            dst_ref=kv_in.at[j, :, slot(2 * d)],
            send_sem=kv_send.at[j, d],
            recv_sem=kv_recv.at[j, d],
            device_id={"seq": partner(d)},
            device_id_type=MESH,
        )

    def fwd_copy(j, d):
        return pltpu.make_async_remote_copy(
            src_ref=kv_in.at[j, :, slot(2 * d)],
            dst_ref=kv_in.at[j, :, slot(2 * d + 1)],
            send_sem=fwd_send.at[j, d],
            recv_sem=fwd_recv.at[j, d],
            device_id={"tile": 1 - c},
            device_id_type=MESH,
        )

    def o_copy(j, d):
        return pltpu.make_async_remote_copy(
            src_ref=o_out.at[j, d],
            dst_ref=att.at[j, d],
            send_sem=o_send.at[j, d],
            recv_sem=o_recv.at[j, d],
            device_id={"seq": partner(d)},
            device_id_type=MESH,
        )

    def x_copy(j, f, d):
        return pltpu.make_async_remote_copy(
            src_ref=att.at[j, d],
            dst_ref=att.at[j, f * n + d],
            send_sem=x_send.at[j, f, d],
            recv_sem=x_recv.at[j, f, d],
            device_id={"head": x_ahead(f)},
            device_id_type=MESH,
        )

    def send_kv(j):
        for d in order:
            loads[1, j, d].wait()
            loads[2, j, d].wait()
            kv_copy(j, d).start()
        for t in range(3):
            loads[t, j, 0].wait()
        fwd_copy(j, 0).start()

    def send_q(j):
        for d in order:
            loads[0, j, d].wait()
            q_copy(j, d).start()

    for j in range(min(2, per_chip)):
        send_kv(j)
        send_q(j)

    w_loads = {}
    for j in range(per_chip):
        for f in range(nx):
            for d in range(n):
                head = x_behind(f) * heads_here + partner(d) * per_chip + j
                copy = pltpu.make_async_copy(
                    w_hbm.at[pl.ds(pl.multiple_of(head * HD, HD), HD)],
                    w_buf.at[j, pl.ds((f * n + d) * HD, HD)],
                    w_sem.at[j, f * n + d],
                )
                copy.start()
                w_loads[j, f, d] = copy

    factor = math.log2(math.e) / math.sqrt(HD)

    def attend(j, d):
        scores = lax.dot_general(
            q_in[j, d],
            kv_in[j, 0],
            (((1,), (1,)), ((), ())),
            preferred_element_type=jnp.float32,
        )
        row_max = jnp.max(scores, axis=1, keepdims=True)
        weights = jnp.exp2((scores - row_max) * factor)
        denominator = jnp.sum(weights, axis=1, keepdims=True)
        numerator = jnp.dot(
            weights.astype(jnp.bfloat16), kv_in[j, 1], preferred_element_type=jnp.float32
        )
        return (numerator / denominator).astype(jnp.bfloat16)

    def relay(j):
        for d in order:
            o_copy(j, d).wait_recv()
            for f in range(1, nx):
                x_copy(j, f, d).start()

    width = math.gcd(columns, 512)

    def project(j):
        for f in range(nx):
            for d in range(n):
                w_loads[j, f, d].wait()
                if f:
                    x_copy(j, f, d).wait_recv()
        rows_in = jnp.concatenate([att[j, s] for s in range(nx * n)], axis=1)
        for start in range(0, columns, width):
            cols = slice(start, start + width)
            part = jnp.dot(rows_in, w_buf[j, :, cols], preferred_element_type=jnp.float32)
            out_ref[:, cols] = out_ref[:, cols] + part if j else part

    for j in range(per_chip):
        for d in order:
            kv_copy(j, d).wait_recv()
            fwd_copy(j, d).start()
        if j and j + 1 < per_chip:
            send_kv(j + 1)
        for d in range(n):
            fwd_copy(j, d).wait_recv()
        att[j, 0] = attend(j, 0)
        for f in range(1, nx):
            x_copy(j, f, 0).start()
        if j and j + 1 == per_chip:
            relay(j - 1)

        def step(i, carry):
            d = n - 1 - i
            q_copy(j, d).wait_recv()
            o_out[j, d] = attend(j, d)
            o_copy(j, d).start()
            return carry

        lax.fori_loop(0, n - 1, step, 0)
        if j and j + 1 < per_chip:
            send_q(j + 1)
            relay(j - 1)
        if j:
            project(j - 1)
    relay(per_chip - 1)
    project(per_chip - 1)

    for j in range(per_chip):
        for d in range(n):
            fwd_copy(j, d).wait_send()
            if d:
                q_copy(j, d).wait_send()
                kv_copy(j, d).wait_send()
                o_copy(j, d).wait_send()
            for f in range(1, nx):
                x_copy(j, f, d).wait_send()


def exchanged(n, nx, query_states, key_states, value_states, out_weight):
    rows, width = query_states.shape
    columns = out_weight.shape[1]
    per_chip = width // HD // n
    bf16 = jnp.bfloat16
    dma = pltpu.SemaphoreType.DMA
    anywhere = pl.BlockSpec(memory_space=pl.ANY)
    in_vmem = pl.BlockSpec(memory_space=pltpu.VMEM)
    return pl.pallas_call(
        functools.partial(kernel, n, nx, per_chip),
        out_shape=jax.ShapeDtypeStruct((rows, columns), jnp.float32),
        in_specs=[anywhere] * 4,
        out_specs=in_vmem,
        scratch_shapes=[
            pltpu.VMEM((per_chip, n, rows, HD), bf16),
            pltpu.VMEM((per_chip, n, 2, rows, HD), bf16),
            pltpu.VMEM((per_chip, n, rows, HD), bf16),
            pltpu.VMEM((per_chip, 2, 2 * n * rows, HD), bf16),
            pltpu.VMEM((per_chip, n, rows, HD), bf16),
            pltpu.VMEM((per_chip, nx * n, rows, HD), bf16),
            pltpu.VMEM((per_chip, nx * n * HD, columns), bf16),
            dma((3, per_chip, n)),
            dma((per_chip, nx * n)),
            dma((per_chip, n)),
            dma((per_chip, n)),
            dma((per_chip, n)),
            dma((per_chip, n)),
            dma((per_chip, n)),
            dma((per_chip, n)),
            dma((per_chip, n)),
            dma((per_chip, n)),
            dma((per_chip, nx, n)),
            dma((per_chip, nx, n)),
        ],
        compiler_params=pltpu.CompilerParams(
            collective_id=0, has_side_effects=True, vmem_limit_bytes=56 << 20
        ),
    )(query_states, key_states, value_states, out_weight)


def solution(mesh):
    n, nx = mesh.shape["seq"], mesh.shape["head"]

    def per_device(query_states, key_states, value_states, residual, out_weight, gate_scale):
        heads_here = query_states.shape[1] // HD
        if heads_here % n or n & (n - 1) or mesh.shape["tile"] != 2:
            return gathered(
                query_states, key_states, value_states, residual, out_weight, gate_scale
            )
        projected = exchanged(n, nx, query_states, key_states, value_states, out_weight)
        return (residual.astype(jnp.float32) + gate_scale[None, :] * projected).astype(
            jnp.bfloat16
        )

    placed = (
        P(("groups", "seq", "tile"), "head"),
        P(("groups", "seq", "tile"), "head"),
        P(("groups", "seq", "tile"), "head"),
        P(("groups", "seq", "tile"), "head"),
        P(None, "head"),
        P(("groups", "head")),
    )
    return jax.shard_map(
        per_device,
        mesh=mesh,
        in_specs=placed,
        out_specs=P(("groups", "seq", "tile"), "head"),
        check_vma=False,
    )
```

```python
import functools
import math

import jax
import jax.numpy as jnp
from jax import lax
from jax.experimental import pallas as pl
from jax.experimental.pallas import tpu as pltpu
from jax.sharding import PartitionSpec as P

HD = 128
MESH = pl.DeviceIdType.MESH


def gathered(query_states, key_states, value_states, residual, out_weight, gate_scale):
    row_count = query_states.shape[0]
    heads_here = query_states.shape[1] // HD
    score_scale = 1.0 / math.sqrt(HD)
    query_heads = query_states.reshape(row_count, heads_here, HD)
    key_heads = lax.all_gather(key_states, ("seq", "tile"), axis=0, tiled=True).reshape(
        -1, heads_here, HD
    )
    value_heads = lax.all_gather(value_states, ("seq", "tile"), axis=0, tiled=True).reshape(
        -1, heads_here, HD
    )
    scores = (
        jnp.einsum("qhd,khd->hqk", query_heads, key_heads, preferred_element_type=jnp.float32)
        * score_scale
    )
    row_max = jnp.max(scores, axis=2)
    weights = jnp.exp(scores - row_max[:, :, None])
    denominator = jnp.sum(weights, axis=2)
    numerator = jnp.einsum(
        "hqk,khd->qhd",
        weights.astype(jnp.bfloat16),
        value_heads,
        preferred_element_type=jnp.float32,
    )
    attended = (
        (numerator / denominator.T[:, :, None])
        .astype(jnp.bfloat16)
        .reshape(row_count, heads_here * HD)
    )
    projected = jnp.dot(
        lax.all_gather(attended, "head", axis=1, tiled=True),
        out_weight,
        preferred_element_type=jnp.float32,
    )
    return (residual.astype(jnp.float32) + gate_scale[None, :] * projected).astype(jnp.bfloat16)


def kernel(
    n,
    nx,
    per_chip,
    q_hbm,
    k_hbm,
    v_hbm,
    w_hbm,
    out_ref,
    q_out,
    kv_out,
    q_in,
    kv_in,
    o_out,
    att,
    w_buf,
    load_sem,
    w_sem,
    q_send,
    q_recv,
    kv_send,
    kv_recv,
    fwd_send,
    fwd_recv,
    o_send,
    o_recv,
    x_send,
    x_recv,
):
    z = lax.axis_index("seq")
    x = lax.axis_index("head")
    c = lax.axis_index("tile")
    rows = q_hbm.shape[0]
    columns = w_hbm.shape[1]
    heads_here = n * per_chip
    bits = [1 << b for b in range(n.bit_length() - 1)]
    order = [0] + [n - 2, n - 1] * (n > 2) + list(range(1, n - 2 * (n > 2)))
    last = per_chip - 1

    def partner(d):
        return sum(b * (((z // b) + (d // b)) % 2) for b in bits)

    def x_ahead(f):
        return lax.rem(x + f, nx)

    def x_behind(f):
        return lax.rem(x - f + nx, nx)

    def slot(s):
        return pl.ds(s * rows, rows)

    loads = {}
    for j in range(per_chip):
        for d in order[1:] + [0]:
            cols = pl.ds(pl.multiple_of((partner(d) * per_chip + j) * HD, HD), HD)
            if d == 0:
                dsts = (q_in.at[j, 0], kv_in.at[j, 0, slot(0)], kv_in.at[j, 1, slot(0)])
            else:
                dsts = (q_out.at[j, d], kv_out.at[j, d, 0], kv_out.at[j, d, 1])
            for t, (src, dst) in enumerate(zip((q_hbm, k_hbm, v_hbm), dsts)):
                copy = pltpu.make_async_copy(src.at[:, cols], dst, load_sem.at[t, j, d])
                copy.start()
                loads[t, j, d] = copy

    barrier = pltpu.get_barrier_semaphore()
    for d in range(1, n):
        pl.semaphore_signal(barrier, inc=1, device_id={"seq": partner(d)}, device_id_type=MESH)
    for f in range(1, nx):
        pl.semaphore_signal(barrier, inc=1, device_id={"head": x_ahead(f)}, device_id_type=MESH)
    pl.semaphore_signal(barrier, inc=1, device_id={"tile": 1 - c}, device_id_type=MESH)
    pl.semaphore_wait(barrier, n + nx - 1)

    def q_copy(j, d):
        return pltpu.make_async_remote_copy(
            src_ref=q_out.at[j, d],
            dst_ref=q_in.at[j, d],
            send_sem=q_send.at[j, d],
            recv_sem=q_recv.at[j, d],
            device_id={"seq": partner(d)},
            device_id_type=MESH,
        )

    def kv_copy(j, d):
        return pltpu.make_async_remote_copy(
            src_ref=kv_out.at[j, d],
            dst_ref=kv_in.at[j, :, slot(2 * d)],
            send_sem=kv_send.at[j, d],
            recv_sem=kv_recv.at[j, d],
            device_id={"seq": partner(d)},
            device_id_type=MESH,
        )

    def fwd_copy(j, d):
        return pltpu.make_async_remote_copy(
            src_ref=kv_in.at[j, :, slot(2 * d)],
            dst_ref=kv_in.at[j, :, slot(2 * d + 1)],
            send_sem=fwd_send.at[j, d],
            recv_sem=fwd_recv.at[j, d],
            device_id={"tile": 1 - c},
            device_id_type=MESH,
        )

    def o_copy(j, p, d):
        return pltpu.make_async_remote_copy(
            src_ref=o_out.at[j, d],
            dst_ref=att.at[j, p * nx],
            send_sem=o_send.at[j, d],
            recv_sem=o_recv.at[j, d],
            device_id={"seq": partner(d)},
            device_id_type=MESH,
        )

    def x_copy(j, f, p):
        return pltpu.make_async_remote_copy(
            src_ref=att.at[j, p * nx],
            dst_ref=att.at[j, p * nx + f],
            send_sem=x_send.at[j, f, p],
            recv_sem=x_recv.at[j, f, p],
            device_id={"head": x_ahead(f)},
            device_id_type=MESH,
        )

    def send_kv(j):
        for d in order[1:]:
            loads[1, j, d].wait()
            loads[2, j, d].wait()
            kv_copy(j, d).start()
        for t in range(3):
            loads[t, j, 0].wait()
        fwd_copy(j, 0).start()

    def send_q(j):
        for d in order[1:]:
            loads[0, j, d].wait()
            q_copy(j, d).start()

    for j in range(min(2, per_chip)):
        send_kv(j)
        send_q(j)

    w_loads = {}
    for j in range(per_chip):
        for p, d in enumerate(order):
            for f in range(nx):
                head = x_behind(f) * heads_here + partner(d) * per_chip + j
                copy = pltpu.make_async_copy(
                    w_hbm.at[pl.ds(pl.multiple_of(head * HD, HD), HD)],
                    w_buf.at[j, pl.ds((p * nx + f) * HD, HD)],
                    w_sem.at[j, p * nx + f],
                )
                copy.start()
                w_loads[j, p, f] = copy

    factor = math.log2(math.e) / math.sqrt(HD)

    def attend(j, d):
        scores = lax.dot_general(
            q_in[j, d],
            kv_in[j, 0],
            (((1,), (1,)), ((), ())),
            preferred_element_type=jnp.float32,
        )
        row_max = jnp.max(scores, axis=1, keepdims=True)
        weights = jnp.exp2((scores - row_max) * factor)
        denominator = jnp.sum(weights, axis=1, keepdims=True)
        numerator = jnp.dot(
            weights.astype(jnp.bfloat16), kv_in[j, 1], preferred_element_type=jnp.float32
        )
        return (numerator / denominator).astype(jnp.bfloat16)

    def relay(j, places=range(1, n)):
        for p in places:
            o_copy(j, p, order[p]).wait_recv()
            for f in range(1, nx):
                x_copy(j, f, p).start()

    width = math.gcd(columns, 512)

    def project(j, low=0, high=n):
        for p in range(low, high):
            for f in range(nx):
                w_loads[j, p, f].wait()
                if f:
                    x_copy(j, f, p).wait_recv()
        rows_in = jnp.concatenate([att[j, s] for s in range(low * nx, high * nx)], axis=1)
        for start in range(0, columns, width):
            cols = slice(start, start + width)
            part = jnp.dot(
                rows_in,
                w_buf[j, low * nx * HD : high * nx * HD, cols],
                preferred_element_type=jnp.float32,
            )
            out_ref[:, cols] = out_ref[:, cols] + part if j or low else part

    for j in range(per_chip):
        for d in order[1:]:
            kv_copy(j, d).wait_recv()
            fwd_copy(j, d).start()
        if j and j < last:
            send_kv(j + 1)
        for d in range(n):
            fwd_copy(j, d).wait_recv()
        att[j, 0] = attend(j, 0)
        for f in range(1, nx):
            x_copy(j, f, 0).start()
        if j and j == last:
            relay(j - 1)

        def step(i, carry):
            d = 1 + (n - 3 + i) % (n - 1) if n > 2 else 1
            q_copy(j, d).wait_recv()
            o_out[j, d] = attend(j, d)
            o_copy(j, i + 1, d).start()
            return carry

        lax.fori_loop(0, n - 1, step, 0)
        if j and j < last:
            send_q(j + 1)
            relay(j - 1)
        if j and j < last:
            project(j - 1)
    if last:
        relay(last, range(1, 2))
        project(last - 1)
        relay(last, range(2, n))
    else:
        relay(last)
    project(last, 0, n - 1)
    project(last, n - 1, n)

    for j in range(per_chip):
        for d in range(n):
            fwd_copy(j, d).wait_send()
            if d:
                q_copy(j, d).wait_send()
                kv_copy(j, d).wait_send()
                o_copy(j, order.index(d), d).wait_send()
            for f in range(1, nx):
                x_copy(j, f, d).wait_send()


def exchanged(n, nx, query_states, key_states, value_states, out_weight):
    rows, width = query_states.shape
    columns = out_weight.shape[1]
    per_chip = width // HD // n
    bf16 = jnp.bfloat16
    dma = pltpu.SemaphoreType.DMA
    anywhere = pl.BlockSpec(memory_space=pl.ANY)
    in_vmem = pl.BlockSpec(memory_space=pltpu.VMEM)
    return pl.pallas_call(
        functools.partial(kernel, n, nx, per_chip),
        out_shape=jax.ShapeDtypeStruct((rows, columns), jnp.float32),
        in_specs=[anywhere] * 4,
        out_specs=in_vmem,
        scratch_shapes=[
            pltpu.VMEM((per_chip, n, rows, HD), bf16),
            pltpu.VMEM((per_chip, n, 2, rows, HD), bf16),
            pltpu.VMEM((per_chip, n, rows, HD), bf16),
            pltpu.VMEM((per_chip, 2, 2 * n * rows, HD), bf16),
            pltpu.VMEM((per_chip, n, rows, HD), bf16),
            pltpu.VMEM((per_chip, nx * n, rows, HD), bf16),
            pltpu.VMEM((per_chip, nx * n * HD, columns), bf16),
            dma((3, per_chip, n)),
            dma((per_chip, nx * n)),
            dma((per_chip, n)),
            dma((per_chip, n)),
            dma((per_chip, n)),
            dma((per_chip, n)),
            dma((per_chip, n)),
            dma((per_chip, n)),
            dma((per_chip, n)),
            dma((per_chip, n)),
            dma((per_chip, nx, n)),
            dma((per_chip, nx, n)),
        ],
        compiler_params=pltpu.CompilerParams(
            collective_id=0, has_side_effects=True, vmem_limit_bytes=56 << 20
        ),
    )(query_states, key_states, value_states, out_weight)


def solution(mesh):
    n, nx = mesh.shape["seq"], mesh.shape["head"]

    def per_device(query_states, key_states, value_states, residual, out_weight, gate_scale):
        heads_here = query_states.shape[1] // HD
        if heads_here % n or n & (n - 1) or mesh.shape["tile"] != 2:
            return gathered(
                query_states, key_states, value_states, residual, out_weight, gate_scale
            )
        projected = exchanged(n, nx, query_states, key_states, value_states, out_weight)
        return (residual.astype(jnp.float32) + gate_scale[None, :] * projected).astype(
            jnp.bfloat16
        )

    placed = (
        P(("groups", "seq", "tile"), "head"),
        P(("groups", "seq", "tile"), "head"),
        P(("groups", "seq", "tile"), "head"),
        P(("groups", "seq", "tile"), "head"),
        P(None, "head"),
        P(("groups", "head")),
    )
    return jax.shard_map(
        per_device,
        mesh=mesh,
        in_specs=placed,
        out_specs=P(("groups", "seq", "tile"), "head"),
        check_vma=False,
    )
```

```python
import functools
import math

import jax
import jax.numpy as jnp
from jax import lax
from jax.experimental import pallas as pl
from jax.experimental.pallas import tpu as pltpu
from jax.sharding import PartitionSpec as P

HD = 128
MESH = pl.DeviceIdType.MESH


def gathered(query_states, key_states, value_states, residual, out_weight, gate_scale):
    row_count = query_states.shape[0]
    heads_here = query_states.shape[1] // HD
    score_scale = 1.0 / math.sqrt(HD)
    query_heads = query_states.reshape(row_count, heads_here, HD)
    key_heads = lax.all_gather(key_states, ("seq", "tile"), axis=0, tiled=True).reshape(
        -1, heads_here, HD
    )
    value_heads = lax.all_gather(value_states, ("seq", "tile"), axis=0, tiled=True).reshape(
        -1, heads_here, HD
    )
    scores = (
        jnp.einsum("qhd,khd->hqk", query_heads, key_heads, preferred_element_type=jnp.float32)
        * score_scale
    )
    row_max = jnp.max(scores, axis=2)
    weights = jnp.exp(scores - row_max[:, :, None])
    denominator = jnp.sum(weights, axis=2)
    numerator = jnp.einsum(
        "hqk,khd->qhd",
        weights.astype(jnp.bfloat16),
        value_heads,
        preferred_element_type=jnp.float32,
    )
    attended = (
        (numerator / denominator.T[:, :, None])
        .astype(jnp.bfloat16)
        .reshape(row_count, heads_here * HD)
    )
    projected = jnp.dot(
        lax.all_gather(attended, "head", axis=1, tiled=True),
        out_weight,
        preferred_element_type=jnp.float32,
    )
    return (residual.astype(jnp.float32) + gate_scale[None, :] * projected).astype(jnp.bfloat16)


def kernel(
    n,
    nx,
    per_chip,
    q_hbm,
    k_hbm,
    v_hbm,
    w_hbm,
    res_hbm,
    gate_hbm,
    out_ref,
    q_out,
    kv_out,
    q_in,
    kv_in,
    o_out,
    att,
    w_buf,
    res_buf,
    gate_buf,
    acc,
    load_sem,
    w_sem,
    end_sem,
    q_send,
    q_recv,
    kv_send,
    kv_recv,
    fwd_send,
    fwd_recv,
    o_send,
    o_recv,
    x_send,
    x_recv,
):
    z = lax.axis_index("seq")
    x = lax.axis_index("head")
    c = lax.axis_index("tile")
    rows = q_hbm.shape[0]
    columns = w_hbm.shape[1]
    heads_here = n * per_chip
    bits = [1 << b for b in range(n.bit_length() - 1)]
    order = [0] + [n - 2, n - 1] * (n > 2) + list(range(1, n - 2 * (n > 2)))
    last = per_chip - 1

    def partner(d):
        return sum(b * (((z // b) + (d // b)) % 2) for b in bits)

    def x_ahead(f):
        return lax.rem(x + f, nx)

    def x_behind(f):
        return lax.rem(x - f + nx, nx)

    def slot(s):
        return pl.ds(s * rows, rows)

    loads = {}
    for j in range(per_chip):
        for d in order[1:] + [0]:
            cols = pl.ds(pl.multiple_of((partner(d) * per_chip + j) * HD, HD), HD)
            if d == 0:
                dsts = (q_in.at[j, 0], kv_in.at[j, 0, slot(0)], kv_in.at[j, 1, slot(0)])
            else:
                dsts = (q_out.at[j, d], kv_out.at[j, d, 0], kv_out.at[j, d, 1])
            for t, (src, dst) in enumerate(zip((q_hbm, k_hbm, v_hbm), dsts)):
                copy = pltpu.make_async_copy(src.at[:, cols], dst, load_sem.at[t, j, d])
                copy.start()
                loads[t, j, d] = copy

    barrier = pltpu.get_barrier_semaphore()
    for d in range(1, n):
        pl.semaphore_signal(barrier, inc=1, device_id={"seq": partner(d)}, device_id_type=MESH)
    for f in range(1, nx):
        pl.semaphore_signal(barrier, inc=1, device_id={"head": x_ahead(f)}, device_id_type=MESH)
    pl.semaphore_signal(barrier, inc=1, device_id={"tile": 1 - c}, device_id_type=MESH)
    pl.semaphore_wait(barrier, n + nx - 1)

    def q_copy(j, d):
        return pltpu.make_async_remote_copy(
            src_ref=q_out.at[j, d],
            dst_ref=q_in.at[j, d],
            send_sem=q_send.at[j, d],
            recv_sem=q_recv.at[j, d],
            device_id={"seq": partner(d)},
            device_id_type=MESH,
        )

    def kv_copy(j, d):
        return pltpu.make_async_remote_copy(
            src_ref=kv_out.at[j, d],
            dst_ref=kv_in.at[j, :, slot(2 * d)],
            send_sem=kv_send.at[j, d],
            recv_sem=kv_recv.at[j, d],
            device_id={"seq": partner(d)},
            device_id_type=MESH,
        )

    def fwd_copy(j, d):
        return pltpu.make_async_remote_copy(
            src_ref=kv_in.at[j, :, slot(2 * d)],
            dst_ref=kv_in.at[j, :, slot(2 * d + 1)],
            send_sem=fwd_send.at[j, d],
            recv_sem=fwd_recv.at[j, d],
            device_id={"tile": 1 - c},
            device_id_type=MESH,
        )

    def o_copy(j, p, d):
        return pltpu.make_async_remote_copy(
            src_ref=o_out.at[j, d],
            dst_ref=att.at[j, p * nx],
            send_sem=o_send.at[j, d],
            recv_sem=o_recv.at[j, d],
            device_id={"seq": partner(d)},
            device_id_type=MESH,
        )

    def x_copy(j, f, p):
        return pltpu.make_async_remote_copy(
            src_ref=att.at[j, p * nx],
            dst_ref=att.at[j, p * nx + f],
            send_sem=x_send.at[j, f, p],
            recv_sem=x_recv.at[j, f, p],
            device_id={"head": x_ahead(f)},
            device_id_type=MESH,
        )

    def send_kv(j):
        for d in order[1:]:
            loads[1, j, d].wait()
            loads[2, j, d].wait()
            kv_copy(j, d).start()
        for t in range(3):
            loads[t, j, 0].wait()
        fwd_copy(j, 0).start()

    def send_q(j):
        for d in order[1:]:
            loads[0, j, d].wait()
            q_copy(j, d).start()

    for j in range(min(2, per_chip)):
        send_kv(j)
        send_q(j)

    w_loads = {}
    for j in range(per_chip):
        for p, d in enumerate(order):
            for f in range(nx):
                head = x_behind(f) * heads_here + partner(d) * per_chip + j
                copy = pltpu.make_async_copy(
                    w_hbm.at[pl.ds(pl.multiple_of(head * HD, HD), HD)],
                    w_buf.at[j, pl.ds((p * nx + f) * HD, HD)],
                    w_sem.at[j, p * nx + f],
                )
                copy.start()
                w_loads[j, p, f] = copy

    ends = [
        pltpu.make_async_copy(res_hbm, res_buf, end_sem.at[0]),
        pltpu.make_async_copy(gate_hbm, gate_buf, end_sem.at[1]),
    ]
    for copy in ends:
        copy.start()

    factor = math.log2(math.e) / math.sqrt(HD)

    def attend(j, d):
        scores = lax.dot_general(
            q_in[j, d],
            kv_in[j, 0],
            (((1,), (1,)), ((), ())),
            preferred_element_type=jnp.float32,
        )
        row_max = jnp.max(scores, axis=1, keepdims=True)
        weights = jnp.exp2((scores - row_max) * factor)
        denominator = jnp.sum(weights, axis=1, keepdims=True)
        numerator = jnp.dot(
            weights.astype(jnp.bfloat16), kv_in[j, 1], preferred_element_type=jnp.float32
        )
        return (numerator / denominator).astype(jnp.bfloat16)

    def relay(j, places=range(1, n)):
        for p in places:
            o_copy(j, p, order[p]).wait_recv()
            for f in range(1, nx):
                x_copy(j, f, p).start()

    width = math.gcd(columns, 512)

    def project(j, low=0, high=n):
        for p in range(low, high):
            for f in range(nx):
                w_loads[j, p, f].wait()
                if f:
                    x_copy(j, f, p).wait_recv()
        rows_in = jnp.concatenate([att[j, s] for s in range(low * nx, high * nx)], axis=1)
        for start in range(0, columns, width):
            cols = slice(start, start + width)
            part = jnp.dot(
                rows_in,
                w_buf[j, low * nx * HD : high * nx * HD, cols],
                preferred_element_type=jnp.float32,
            )
            total = acc[:, cols] + part if j or low else part
            if j == last and high == n:
                gate = gate_buf[cols].reshape(1, width)
                out_ref[:, cols] = (
                    res_buf[:, cols].astype(jnp.float32) + gate * total
                ).astype(jnp.bfloat16)
            else:
                acc[:, cols] = total

    for j in range(per_chip):
        for d in order[1:]:
            kv_copy(j, d).wait_recv()
            fwd_copy(j, d).start()
        if j and j < last:
            send_kv(j + 1)
        for d in range(n):
            fwd_copy(j, d).wait_recv()
        att[j, 0] = attend(j, 0)
        for f in range(1, nx):
            x_copy(j, f, 0).start()

        follow = j and j < last
        if follow:
            for d in order[1:]:
                loads[0, j + 1, d].wait()

        def step(i, carry):
            d = 1 + (n - 3 + i) % (n - 1) if n > 2 else 1
            if j and j == last:
                o_copy(j - 1, i + 1, d).wait_recv()
                for f in range(1, nx):
                    x_copy(j - 1, f, i + 1).start()
            q_copy(j, d).wait_recv()
            o_out[j, d] = attend(j, d)
            o_copy(j, i + 1, d).start()
            if follow:
                q_copy(j + 1, d).start()
            return carry

        lax.fori_loop(0, n - 1, step, 0)
        if j and j < last:
            relay(j - 1)
        if j and j < last:
            project(j - 1)
    if last:
        relay(last, range(1, 2))
        project(last - 1)
        relay(last, range(2, n))
    else:
        relay(last)
    project(last, 0, n - 1)
    for copy in ends:
        copy.wait()
    project(last, n - 1, n)

    for j in range(per_chip):
        for d in range(n):
            fwd_copy(j, d).wait_send()
            if d:
                q_copy(j, d).wait_send()
                kv_copy(j, d).wait_send()
                o_copy(j, order.index(d), d).wait_send()
            for f in range(1, nx):
                x_copy(j, f, d).wait_send()


def exchanged(n, nx, query_states, key_states, value_states, out_weight, residual, gate_scale):
    rows, width = query_states.shape
    columns = out_weight.shape[1]
    per_chip = width // HD // n
    bf16 = jnp.bfloat16
    dma = pltpu.SemaphoreType.DMA
    anywhere = pl.BlockSpec(memory_space=pl.ANY)
    in_vmem = pl.BlockSpec(memory_space=pltpu.VMEM)
    return pl.pallas_call(
        functools.partial(kernel, n, nx, per_chip),
        out_shape=jax.ShapeDtypeStruct((rows, columns), bf16),
        in_specs=[anywhere] * 6,
        out_specs=in_vmem,
        scratch_shapes=[
            pltpu.VMEM((per_chip, n, rows, HD), bf16),
            pltpu.VMEM((per_chip, n, 2, rows, HD), bf16),
            pltpu.VMEM((per_chip, n, rows, HD), bf16),
            pltpu.VMEM((per_chip, 2, 2 * n * rows, HD), bf16),
            pltpu.VMEM((per_chip, n, rows, HD), bf16),
            pltpu.VMEM((per_chip, nx * n, rows, HD), bf16),
            pltpu.VMEM((per_chip, nx * n * HD, columns), bf16),
            pltpu.VMEM((rows, columns), bf16),
            pltpu.VMEM((columns,), jnp.float32),
            pltpu.VMEM((rows, columns), jnp.float32),
            dma((3, per_chip, n)),
            dma((per_chip, nx * n)),
            dma((2,)),
            dma((per_chip, n)),
            dma((per_chip, n)),
            dma((per_chip, n)),
            dma((per_chip, n)),
            dma((per_chip, n)),
            dma((per_chip, n)),
            dma((per_chip, n)),
            dma((per_chip, n)),
            dma((per_chip, nx, n)),
            dma((per_chip, nx, n)),
        ],
        compiler_params=pltpu.CompilerParams(
            collective_id=0, has_side_effects=True, vmem_limit_bytes=56 << 20
        ),
    )(query_states, key_states, value_states, out_weight, residual, gate_scale)


def solution(mesh):
    n, nx = mesh.shape["seq"], mesh.shape["head"]

    def per_device(query_states, key_states, value_states, residual, out_weight, gate_scale):
        heads_here = query_states.shape[1] // HD
        if heads_here % n or n & (n - 1) or mesh.shape["tile"] != 2:
            return gathered(
                query_states, key_states, value_states, residual, out_weight, gate_scale
            )
        return exchanged(
            n, nx, query_states, key_states, value_states, out_weight, residual, gate_scale
        )

    placed = (
        P(("groups", "seq", "tile"), "head"),
        P(("groups", "seq", "tile"), "head"),
        P(("groups", "seq", "tile"), "head"),
        P(("groups", "seq", "tile"), "head"),
        P(None, "head"),
        P(("groups", "head")),
    )
    return jax.shard_map(
        per_device,
        mesh=mesh,
        in_specs=placed,
        out_specs=P(("groups", "seq", "tile"), "head"),
        check_vma=False,
    )
```
